32 devices in a mesh: cores: 4 (over y, x), mode: 8 (over z, core).
Axes of the slice: x: 2, y: 2, z: 4, core: 2. Of those that a mesh axis runs over, the one named last changes fastest.
Arguments:
- x_cores: bfloat16 [4, 512, 128, 512], P('cores', None, 'mode'), may hold values from -0.25 to 0.25
- y_cores: bfloat16 [4, 256, 128, 256], P('cores', None, 'mode'), may hold values from -40 to 40
- left_boundary: bfloat16 [256, 512], replicated, may hold values from -6 to 6
- right_boundary: bfloat16 [256, 512], replicated, may hold values from -6 to 6
Outputs:
- projected: bfloat16 [4, 256, 128, 256], P('cores', None, 'mode')
The draws below stay inside these ranges and needn't reach their ends.
All inputs are finite; a program needn't handle non-finite values.
Results may differ from the reference program's by a relative error of at most 0.014.
Values may be sent and summed in bfloat16 or wider, within the bound.
A program may use at most 128 MiB of HBM per device.

```python
import math
import jax
import jax.numpy as jnp
from jax import lax

RANK_X = 512
RANK_Y = 256
NCORES = 4
MODES = 128


def draw_y_cores(key, part):
    base_key = jax.random.fold_in(key, 17)
    first_key, second_key, third_key = jax.random.split(base_key, 3)
    shape_full = (NCORES, RANK_Y, MODES, RANK_Y)
    left_scale = jnp.exp(jax.random.uniform(first_key, (NCORES, RANK_Y, 1, 1)) * math.log(10.0))
    right_scale = jnp.exp(jax.random.uniform(second_key, (NCORES, 1, 1, RANK_Y)) * math.log(10.0))
    sampled = jax.random.normal(third_key, shape_full)
    values = jnp.clip(sampled * left_scale * right_scale / math.sqrt(RANK_Y), -40.0, 40.0)
    return values.astype(jnp.bfloat16)


def shard_levels(key, shape, pieces, least, high):
    factor_of = 1.0
    for axis_at, blocks in pieces:
        steps = jax.random.uniform(jax.random.fold_in(jax.random.fold_in(key, 6), axis_at), (blocks,), jnp.float32, least / len(pieces), high / len(pieces))
        factor_of = factor_of * jnp.repeat(jnp.exp(steps), shape[axis_at] // blocks).reshape((-1,) + (1,) * (len(shape) - 1 - axis_at))
    return factor_of


def noise(stream_key, dims, width, bound, cuts=(), kind=jnp.bfloat16):
    factor_of = shard_levels(stream_key, dims, cuts, -0.22, 0.18) if cuts else 1.0
    entries = jax.random.normal(stream_key, dims, jnp.float32) * width * factor_of
    return jnp.minimum(jnp.maximum(entries, -bound), bound).astype(kind)


def setup_inputs(seed: int = 0) -> dict:
    key_of = jax.random.split(jax.random.key(seed), 5)
    return {
        "x_cores": noise(key_of[0], (NCORES, RANK_X, MODES, RANK_X), RANK_X ** -0.5, 0.25, ((0, 4), (2, 8))),
        "y_cores": draw_y_cores(jax.random.fold_in(key_of[4], 71), 0),
        "left_boundary": noise(key_of[2], (RANK_Y, RANK_X), 1.0, 6.0),
        "right_boundary": noise(key_of[3], (RANK_Y, RANK_X), 1.0, 6.0),
    }


epsilon = 1e-06

def normalized(summed):
    return (summed * lax.rsqrt(jnp.mean(summed * summed) + epsilon)).astype(jnp.bfloat16)

def reference(x_cores, y_cores, left_boundary, right_boundary):
    core_count = x_cores.shape[0]
    environ = left_boundary
    applied_list = []
    for core_index in range(core_count):
        source = x_cores[core_index]
        target = y_cores[core_index]
        applied = jnp.dot(environ, source.reshape(RANK_X, MODES * RANK_X), preferred_element_type=jnp.float32).astype(jnp.bfloat16)
        applied_list.append(applied)
        if core_index < core_count - 1:
            summed = lax.dot_general(target.reshape(RANK_Y * MODES, RANK_Y), applied.reshape(RANK_Y * MODES, RANK_X), (((0,), (0,)), ((), ())), preferred_element_type=jnp.float32)
            environ = normalized(summed)
    environ = right_boundary
    results = [None] * core_count
    for core_index in reversed(range(core_count)):
        applied = applied_list[core_index].reshape(RANK_Y * MODES, RANK_X)
        product = lax.dot_general(applied, environ, (((1,), (1,)), ((), ())), preferred_element_type=jnp.float32) * (1.0 / math.sqrt(RANK_X))
        results[core_index] = product.astype(jnp.bfloat16).reshape(RANK_Y, MODES, RANK_Y)
        if core_index > 0:
            source = x_cores[core_index]
            target = y_cores[core_index]
            carried_back = lax.dot_general(source.reshape(RANK_X * MODES, RANK_X), environ, (((1,), (1,)), ((), ())), preferred_element_type=jnp.float32).astype(jnp.bfloat16)
            carried_back = carried_back.reshape(RANK_X, MODES * RANK_Y)
            summed = lax.dot_general(target.reshape(RANK_Y, MODES * RANK_Y), carried_back, (((1,), (1,)), ((), ())), preferred_element_type=jnp.float32)
            environ = normalized(summed)
    return jnp.stack(results)
```

```python
import functools
import math

import jax
import jax.numpy as jnp
from jax import lax
from jax.experimental import pallas as pl
from jax.experimental.pallas import tpu as pltpu
from jax.sharding import PartitionSpec as P

epsilon = 1e-06
f32 = jnp.float32
bf16 = jnp.bfloat16
NN = (((1,), (0,)), ((), ()))
NT = (((1,), (1,)), ((), ()))
TN = (((0,), (0,)), ((), ()))


def dot(a, b, dims):
    return lax.dot_general(a, b, dims, preferred_element_type=f32)


def kernel(groups, chips, x_hbm, y_hbm, lb, rb, out_hbm, xv, yv, keep, outv, env, acc,
           pair_out, pair_in, stage, parts, x_sem, y_sem, o_sem, pair_sem, part_send, part_recv,
           gather_send, gather_recv, relay_send, relay_recv):
    g = lax.axis_index("cores")
    m = lax.axis_index("mode")
    chip = m // 2
    core = lax.rem(m, 2)
    partner = chip * 2 + (1 - core)
    points = xv.shape[0]
    rank_y, rank_x = lb.shape
    half = rank_y // 2
    row_cuts = min(chips, half // 16)
    col_cuts = chips // row_cuts
    rows, cols = half // row_cuts, rank_x // col_cuts
    norm = 1.0 / math.sqrt(rank_x)

    def x_load(i):
        return pltpu.make_async_copy(x_hbm.at[i], xv.at[i], x_sem.at[i])

    def y_load(i):
        return pltpu.make_async_copy(y_hbm.at[i], yv.at[i], y_sem.at[i])

    def out_store(i):
        return pltpu.make_async_copy(outv.at[i], out_hbm.at[i], o_sem.at[i])

    @pl.loop(0, points)
    def _(i):
        x_load(i).start()
        y_load(i).start()

    barrier = pltpu.get_barrier_semaphore()

    def greet(group, index):
        pl.semaphore_signal(barrier, inc=1, device_id=(group, index), device_id_type=pl.DeviceIdType.MESH)

    greet(g, partner)
    for step in range(1, chips):
        greet(g, lax.rem(chip + step, chips) * 2 + core)

    @pl.when(g > 0)
    def _():
        for j in range(chips):
            greet(g - 1, j * 2 + core)

    @pl.when(g < groups - 1)
    def _():
        for j in range(chips):
            greet(g + 1, j * 2 + core)

    sides = jnp.where(g > 0, 1, 0) + jnp.where(g < groups - 1, 1, 0)
    pl.semaphore_wait(barrier, chips * (1 + sides))

    def remote(src, dst, send, recv, group, index):
        return pltpu.make_async_remote_copy(
            src_ref=src, dst_ref=dst, send_sem=send, recv_sem=recv,
            device_id=(group, index), device_id_type=pl.DeviceIdType.MESH,
        )

    def place(j, base):
        if col_cuts == 1:
            return pl.ds(pl.multiple_of(base + j * rows, rows), rows), pl.ds(0, cols)
        return (
            pl.ds(pl.multiple_of(base + (j // col_cuts) * rows, rows), rows),
            pl.ds(pl.multiple_of(lax.rem(j, col_cuts) * cols, cols), cols),
        )

    def produce(d, scale, store, first):
        acc[...] = jnp.zeros_like(acc)

        @pl.loop(0, points)
        def _(i):
            if first:
                x_load(i).wait()
                y_load(i).wait()
            value = (dot(env[d], xv[i], NT if d else NN) * scale).astype(bf16)
            if store:
                keep[i] = value
            acc[...] += dot(yv[i], value, NN if d else TN)

    def part_copy(d, j, group):
        at = place(j, 0)
        return remote(stage.at[d].at[at[0], at[1]], parts.at[d].at[chip], part_send.at[d, j],
                      part_recv.at[d, chip], group, j * 2 + core)

    def pair_copy(d):
        return remote(pair_out.at[d], pair_in.at[d], pair_sem.at[d, 0], pair_sem.at[d, 1], g, partner)

    def dispatch(d, group):
        other = pl.ds(pl.multiple_of((1 - core) * half, half), half)
        own = pl.ds(pl.multiple_of(core * half, half), half)
        pair_out[d] = acc[other, :].astype(bf16)
        copy = pair_copy(d)
        copy.start()
        copy.wait()
        stage[d] = (acc[own, :] + pair_in[d].astype(f32)).astype(bf16)
        for j in range(chips):
            part_copy(d, j, group).start()

    def finish(d, group):
        for j in range(chips):
            part_copy(d, j, group).wait_send()

    def gather_copy(d, owner, target):
        at = place(owner, core * half)
        block = env.at[d].at[at[0], at[1]]
        return remote(block, block, gather_send.at[d, target], gather_recv.at[d, owner], g, target * 2 + core)

    def relay_copy(d, owner, side):
        at = place(owner, side * half)
        block = env.at[d].at[at[0], at[1]]
        return remote(block, block, relay_send.at[d, owner], relay_recv.at[d, owner], g, partner)

    def collect(d, group):
        total = jnp.zeros((rows, cols), f32)
        for j in range(chips):
            at = place(j, 0)
            remote(stage.at[d].at[at[0], at[1]], parts.at[d].at[j], part_send.at[d, j],
                   part_recv.at[d, j], group, j * 2 + core).wait_recv()
            total = total + parts[d, j].astype(f32)
        at = place(chip, core * half)
        env[d, at[0], at[1]] = total.astype(bf16)
        for step in range(1, chips):
            gather_copy(d, chip, lax.rem(chip + step, chips)).start()
        relay_copy(d, chip, core).start()
        for step in range(1, chips):
            owner = lax.rem(chip + step, chips)
            gather_copy(d, owner, owner).wait_recv()
            relay_copy(d, owner, core).start()
        for j in range(chips):
            relay_copy(d, j, 1 - core).wait_recv()
        for step in range(1, chips):
            gather_copy(d, chip, lax.rem(chip + step, chips)).wait_send()
        for j in range(chips):
            relay_copy(d, j, core).wait_send()

    def level(d):
        values = env[d].astype(f32)
        return lax.rsqrt(jnp.mean(values * values) + epsilon)

    def project(d, scale):
        factor = scale * norm

        @pl.loop(0, points)
        def _(i):
            if d:
                value = dot(keep[i], env[1], NT)
            else:
                value = dot(env[0], keep[i], NT)
            outv[i] = (value * factor).astype(bf16)
            out_store(i).start()

        @pl.loop(0, points)
        def _(i):
            out_store(i).wait()

    def run(first, boundary, edge, ahead, far):
        second = 1 - first
        behind = g - (ahead - g)

        @pl.when(g == edge)
        def _():
            env[first] = boundary[...]

        @pl.when(g != edge)
        def _():
            collect(first, behind)

        scale = jnp.where(g == edge, 1.0, level(first))
        produce(first, scale, True, True)
        dispatch(first, ahead)
        finish(first, ahead)
        collect(second, ahead)
        scale = level(second)

        @pl.when(g != edge)
        def _():
            produce(second, scale, False, False)
            dispatch(second, behind)

        project(second, scale)

        @pl.when(g != edge)
        def _():
            finish(second, behind)

    @pl.when(2 * g < groups)
    def _():
        run(0, lb, 0, g + 1, None)

    @pl.when(2 * g >= groups)
    def _():
        run(1, rb, groups - 1, g - 1, None)


def body(groups, members, x_cores, y_cores, left_boundary, right_boundary):
    rank_y, rank_x = left_boundary.shape
    points = x_cores.shape[2]
    chips = members // 2
    half = rank_y // 2
    row_cuts = min(chips, half // 16)
    col_cuts = chips // row_cuts
    rows, cols = half // row_cuts, rank_x // col_cuts
    x = jnp.transpose(x_cores[0], (1, 0, 2))
    y = jnp.transpose(y_cores[0], (1, 0, 2))
    dma = pltpu.SemaphoreType.DMA
    vmem = pl.BlockSpec(memory_space=pltpu.VMEM)
    anywhere = pl.BlockSpec(memory_space=pl.ANY)
    out = pl.pallas_call(
        functools.partial(kernel, groups, chips),
        out_shape=jax.ShapeDtypeStruct((points, rank_y, rank_y), bf16),
        in_specs=[anywhere, anywhere, vmem, vmem],
        out_specs=anywhere,
        scratch_shapes=[
            pltpu.VMEM((points, rank_x, rank_x), bf16),
            pltpu.VMEM((points, rank_y, rank_y), bf16),
            pltpu.VMEM((points, rank_y, rank_x), bf16),
            pltpu.VMEM((points, rank_y, rank_y), bf16),
            pltpu.VMEM((2, rank_y, rank_x), bf16),
            pltpu.VMEM((rank_y, rank_x), f32),
            pltpu.VMEM((2, half, rank_x), bf16),
            pltpu.VMEM((2, half, rank_x), bf16),
            pltpu.VMEM((2, half, rank_x), bf16),
            pltpu.VMEM((2, chips, rows, cols), bf16),
            dma((points,)), dma((points,)), dma((points,)), dma((2, 2)),
            dma((2, chips)), dma((2, chips)), dma((2, chips)), dma((2, chips)), dma((2, chips)), dma((2, chips)),
        ],
        compiler_params=pltpu.CompilerParams(
            collective_id=0, has_side_effects=True, vmem_limit_bytes=48 * 1024 * 1024
        ),
    )(x, y, left_boundary, right_boundary)
    return jnp.transpose(out, (1, 0, 2))[None]


def solution(mesh):
    in_specs = (P("cores", None, "mode", None), P("cores", None, "mode", None), P(), P())
    out_specs = P("cores", None, "mode", None)
    fn = functools.partial(body, mesh.shape["cores"], mesh.shape["mode"])
    return jax.shard_map(fn, mesh=mesh, in_specs=in_specs, out_specs=out_specs, check_vma=False)
```

```python
import functools
import math

import jax
import jax.numpy as jnp
from jax import lax
from jax.experimental import pallas as pl
from jax.experimental.pallas import tpu as pltpu
from jax.sharding import PartitionSpec as P

epsilon = 1e-06
f32 = jnp.float32
bf16 = jnp.bfloat16
chunk = 64
NN = (((1,), (0,)), ((), ()))
NT = (((1,), (1,)), ((), ()))
TN = (((0,), (0,)), ((), ()))


def dot(a, b, dims):
    return lax.dot_general(a, b, dims, preferred_element_type=f32)


def cuts(chips, rank_y, rank_x):
    half = rank_y // 2
    row_cuts = min(chips, half // 16)
    col_cuts = chips // row_cuts
    splits = 1
    width = rank_x // splits
    return half, splits, width, half // row_cuts, width // col_cuts, col_cuts


def kernel(groups, chips, x_hbm, y_hbm, lb, rb, outv, xin, yin, xv, yv, keep, env, acc,
           pair_out, pair_in, stage, parts, level, x_sem, y_sem, pair_send, pair_recv, part_send, part_recv,
           gather_send, gather_recv, relay_send, relay_recv):
    g = lax.axis_index("cores")
    m = lax.axis_index("mode")
    chip = m // 2
    core = lax.rem(m, 2)
    partner = chip * 2 + (1 - core)
    points = xv.shape[0]
    rank_y, rank_x = lb.shape
    half, splits, width, rows, cols, col_cuts = cuts(chips, rank_y, rank_x)
    batch = math.gcd(points, 8)
    batches = points // batch
    norm = 1.0 / math.sqrt(rank_x)

    def load(source, target, sem, j):
        at = pl.ds(pl.multiple_of(j * chunk, chunk), chunk)
        return pltpu.make_async_copy(source.at[at], target.at[at], sem.at[j])

    for j in range(rank_x // chunk):
        load(x_hbm, xin, x_sem, j).start()
    for j in range(rank_y // chunk):
        load(y_hbm, yin, y_sem, j).start()

    def turn(source, held, target, sem):
        @pl.loop(0, source.shape[0] // chunk)
        def _(j):
            load(source, held, sem, j).wait()
            for r in range(0, chunk, 16):
                at = pl.ds(pl.multiple_of(j * chunk + r, 16), 16)
                for c in range(0, source.shape[2], 128):
                    target[:, at, c:c + 128] = jnp.swapaxes(held[at, :, c:c + 128], 0, 1)

    barrier = pltpu.get_barrier_semaphore()

    def greet(group, index):
        pl.semaphore_signal(barrier, inc=1, device_id=(group, index), device_id_type=pl.DeviceIdType.MESH)

    greet(g, partner)
    for step in range(1, chips):
        greet(g, lax.rem(chip + step, chips) * 2 + core)

    @pl.when(g > 0)
    def _():
        for j in range(chips):
            greet(g - 1, j * 2 + core)

    @pl.when(g < groups - 1)
    def _():
        for j in range(chips):
            greet(g + 1, j * 2 + core)

    turn(x_hbm, xin, xv, x_sem)
    turn(y_hbm, yin, yv, y_sem)
    sides = jnp.where(g > 0, 1, 0) + jnp.where(g < groups - 1, 1, 0)
    pl.semaphore_wait(barrier, chips * (1 + sides))

    def remote(src, dst, send, recv, group, index):
        return pltpu.make_async_remote_copy(
            src_ref=src, dst_ref=dst, send_sem=send, recv_sem=recv,
            device_id=(group, index), device_id_type=pl.DeviceIdType.MESH,
        )

    def place(j, base, side):
        if col_cuts == 1:
            return pl.ds(pl.multiple_of(base + j * rows, rows), rows), pl.ds(side, cols)
        return (
            pl.ds(pl.multiple_of(base + (j // col_cuts) * rows, rows), rows),
            pl.ds(pl.multiple_of(side + lax.rem(j, col_cuts) * cols, cols), cols),
        )

    def produce(d, h, scale, store, lo, hi):
        at = pl.ds(h * width, width)

        @pl.loop(lo, hi)
        def _(k):
            summed = None
            for u in range(batch):
                i = k * batch + u
                if d:
                    value = dot(env[1], xv[i, at, :], NT)
                else:
                    value = dot(env[0], xv[i, :, at], NN)
                value = (value * scale).astype(bf16)
                if store:
                    keep[i, :, at] = value
                term = dot(yv[i], value, NN if d else TN)
                summed = term if summed is None else summed + term
            acc[h] += summed

    def part_copy(d, h, j, slot, group):
        at = place(j, 0, 0)
        return remote(stage.at[d, h].at[at[0], at[1]], parts.at[d, h].at[slot], part_send.at[d, h, j],
                      part_recv.at[d, h, slot], group, j * 2 + core)

    def pair_copy(d, h):
        return remote(pair_out.at[d, h], pair_in.at[d, h], pair_send.at[d, h], pair_recv.at[d, h], g, partner)

    def pair_start(d, h):
        other = pl.ds(pl.multiple_of((1 - core) * half, half), half)
        pair_out[d, h] = acc[h, other, :].astype(bf16)
        pair_copy(d, h).start()

    def part_start(d, h, group):
        own = pl.ds(pl.multiple_of(core * half, half), half)
        pair_copy(d, h).wait_recv()
        stage[d, h] = (acc[h, own, :] + pair_in[d, h].astype(f32)).astype(bf16)
        for j in range(chips):
            part_copy(d, h, j, chip, group).start()

    def advance(d, scale, store, group):
        acc[...] = jnp.zeros_like(acc)
        for h in range(splits):
            if h:
                produce(d, h, scale, store, 0, batches // 2)
                part_start(d, h - 1, group)
                produce(d, h, scale, store, batches // 2, batches)
            else:
                produce(d, h, scale, store, 0, batches)
            pair_start(d, h)
        part_start(d, splits - 1, group)

    def finish(d, group):
        for h in range(splits):
            pair_copy(d, h).wait_send()
            for j in range(chips):
                part_copy(d, h, j, chip, group).wait_send()

    def gather_copy(d, h, owner, target):
        at = place(owner, core * half, h * width)
        block = env.at[d].at[at[0], at[1]]
        return remote(block, block, gather_send.at[d, h, target], gather_recv.at[d, h, owner], g, target * 2 + core)

    def relay_copy(d, h, owner, side):
        at = place(owner, side * half, h * width)
        block = env.at[d].at[at[0], at[1]]
        return remote(block, block, relay_send.at[d, h, owner], relay_recv.at[d, h, owner], g, partner)

    def collect(d, group):
        squares = 0.0
        for h in range(splits):
            total = jnp.zeros((rows, cols), f32)
            for j in range(chips):
                part_copy(d, h, j, j, group).wait_recv()
                total = total + parts[d, h, j].astype(f32)
            at = place(chip, core * half, h * width)
            env[d, at[0], at[1]] = total.astype(bf16)
            for step in range(1, chips):
                gather_copy(d, h, chip, lax.rem(chip + step, chips)).start()
            relay_copy(d, h, chip, core).start()
            for step in range(1, chips):
                owner = lax.rem(chip + step, chips)
                gather_copy(d, h, owner, owner).wait_recv()
                relay_copy(d, h, owner, core).start()
            for j in range(chips):
                relay_copy(d, h, j, 1 - core).wait_recv()
            values = env[d, :, pl.ds(h * width, width)].astype(f32)
            squares = squares + jnp.sum(values * values)
        for h in range(splits):
            for step in range(1, chips):
                gather_copy(d, h, chip, lax.rem(chip + step, chips)).wait_send()
            for j in range(chips):
                relay_copy(d, h, j, core).wait_send()
        return lax.rsqrt(squares / (rank_y * rank_x) + epsilon)

    def project(d, scale):
        factor = scale * norm

        @pl.loop(0, batches)
        def _(k):
            group = pl.ds(k * batch, batch)
            if d:
                value = dot(keep[group].reshape(batch * rank_y, rank_x), env[1], NT) * factor
                outv[group] = value.astype(bf16).reshape(batch, rank_y, rank_y)
            else:
                for u in range(batch):
                    outv[k * batch + u] = (dot(env[0], keep[k * batch + u], NT) * factor).astype(bf16)

    def run(first, boundary, edge, ahead):
        second = 1 - first
        behind = g - (ahead - g)

        @pl.when(g == edge)
        def _():
            env[first] = boundary[...]
            level[0] = 1.0

        @pl.when(g != edge)
        def _():
            level[0] = collect(first, behind)

        advance(first, level[0], True, ahead)
        finish(first, ahead)
        scale = collect(second, ahead)

        @pl.when(g != edge)
        def _():
            advance(second, scale, False, behind)

        project(second, scale)

        @pl.when(g != edge)
        def _():
            finish(second, behind)

    @pl.when(2 * g < groups)
    def _():
        run(0, lb, 0, g + 1)

    @pl.when(2 * g >= groups)
    def _():
        run(1, rb, groups - 1, g - 1)


def body(groups, members, x_cores, y_cores, left_boundary, right_boundary):
    rank_y, rank_x = left_boundary.shape
    points = x_cores.shape[2]
    chips = members // 2
    half, splits, width, rows, cols, col_cuts = cuts(chips, rank_y, rank_x)
    dma = pltpu.SemaphoreType.DMA
    vmem = pl.BlockSpec(memory_space=pltpu.VMEM)
    anywhere = pl.BlockSpec(memory_space=pl.ANY)
    out = pl.pallas_call(
        functools.partial(kernel, groups, chips),
        out_shape=jax.ShapeDtypeStruct((points, rank_y, rank_y), bf16),
        in_specs=[anywhere, anywhere, vmem, vmem],
        out_specs=vmem,
        scratch_shapes=[
            pltpu.VMEM((rank_x, points, rank_x), bf16),
            pltpu.VMEM((rank_y, points, rank_y), bf16),
            pltpu.VMEM((points, rank_x, rank_x), bf16),
            pltpu.VMEM((points, rank_y, rank_y), bf16),
            pltpu.VMEM((points, rank_y, rank_x), bf16),
            pltpu.VMEM((2, rank_y, rank_x), bf16),
            pltpu.VMEM((splits, rank_y, width), f32),
            pltpu.VMEM((2, splits, half, width), bf16),
            pltpu.VMEM((2, splits, half, width), bf16),
            pltpu.VMEM((2, splits, half, width), bf16),
            pltpu.VMEM((2, splits, chips, rows, cols), bf16),
            pltpu.SMEM((1,), f32),
            dma((rank_x // chunk,)), dma((rank_y // chunk,)), dma((2, splits)), dma((2, splits)),
            dma((2, splits, chips)), dma((2, splits, chips)), dma((2, splits, chips)),
            dma((2, splits, chips)), dma((2, splits, chips)), dma((2, splits, chips)),
        ],
        compiler_params=pltpu.CompilerParams(
            collective_id=0, has_side_effects=True, vmem_limit_bytes=48 * 1024 * 1024
        ),
    )(x_cores[0], y_cores[0], left_boundary, right_boundary)
    return jnp.transpose(out, (1, 0, 2))[None]


def solution(mesh):
    in_specs = (P("cores", None, "mode", None), P("cores", None, "mode", None), P(), P())
    out_specs = P("cores", None, "mode", None)
    fn = functools.partial(body, mesh.shape["cores"], mesh.shape["mode"])
    return jax.shard_map(fn, mesh=mesh, in_specs=in_specs, out_specs=out_specs, check_vma=False)
```

```python
import functools
import math

import jax
import jax.numpy as jnp
from jax import lax
from jax.experimental import pallas as pl
from jax.experimental.pallas import tpu as pltpu
from jax.sharding import PartitionSpec as P

epsilon = 1e-06
f32 = jnp.float32
bf16 = jnp.bfloat16
chunk = 64
NN = (((1,), (0,)), ((), ()))
NT = (((1,), (1,)), ((), ()))
TN = (((0,), (0,)), ((), ()))


def dot(a, b, dims):
    return lax.dot_general(a, b, dims, preferred_element_type=f32)


def cuts(chips, rank_y, rank_x):
    half = rank_y // 2
    row_cuts = min(chips, half // 16)
    col_cuts = chips // row_cuts
    splits = 2 if rank_x // 2 // col_cuts >= 128 else 1
    width = rank_x // splits
    return half, splits, width, half // row_cuts, width // col_cuts, col_cuts


def kernel(groups, chips, x_hbm, y_hbm, lb, rb, out_hbm, outv, xin, yin, xv, yv, keep, env, acc,
           pair_out, pair_in, stage, parts, level, x_sem, y_sem, b_sem, o_sem, pair_send, pair_recv, part_send, part_recv,
           gather_send, gather_recv, relay_send, relay_recv):
    g = lax.axis_index("cores")
    m = lax.axis_index("mode")
    chip = m // 2
    core = lax.rem(m, 2)
    partner = chip * 2 + (1 - core)
    points = xv.shape[0]
    rank_y, rank_x = lb.shape
    half, splits, width, rows, cols, col_cuts = cuts(chips, rank_y, rank_x)
    batch = math.gcd(points, 8)
    batches = points // batch
    norm = 1.0 / math.sqrt(rank_x)

    def load(source, target, sem, j):
        at = pl.ds(pl.multiple_of(j * chunk, chunk), chunk)
        return pltpu.make_async_copy(source.at[at], target.at[at], sem.at[j])

    for j in range(rank_x // chunk):
        load(x_hbm, xin, x_sem, j).start()
    for j in range(rank_y // chunk):
        load(y_hbm, yin, y_sem, j).start()

    def bound(d):
        return pltpu.make_async_copy(rb if d else lb, env.at[d], b_sem)

    @pl.when(g == 0)
    def _():
        bound(0).start()

    @pl.when(g == groups - 1)
    def _():
        bound(1).start()

    def turn(source, held, target, sem):
        @pl.loop(0, source.shape[0] // chunk)
        def _(j):
            load(source, held, sem, j).wait()
            for r in range(0, chunk, 16):
                at = pl.ds(pl.multiple_of(j * chunk + r, 16), 16)
                for c in range(0, source.shape[2], 128):
                    target[:, at, c:c + 128] = jnp.swapaxes(held[at, :, c:c + 128], 0, 1)

    barrier = pltpu.get_barrier_semaphore()

    def greet(group, index):
        pl.semaphore_signal(barrier, inc=1, device_id=(group, index), device_id_type=pl.DeviceIdType.MESH)

    greet(g, partner)
    for step in range(1, chips):
        greet(g, lax.rem(chip + step, chips) * 2 + core)

    @pl.when(g > 0)
    def _():
        for j in range(chips):
            greet(g - 1, j * 2 + core)

    @pl.when(g < groups - 1)
    def _():
        for j in range(chips):
            greet(g + 1, j * 2 + core)

    turn(x_hbm, xin, xv, x_sem)
    turn(y_hbm, yin, yv, y_sem)
    sides = jnp.where(g > 0, 1, 0) + jnp.where(g < groups - 1, 1, 0)
    pl.semaphore_wait(barrier, chips * (1 + sides))

    def remote(src, dst, send, recv, group, index):
        return pltpu.make_async_remote_copy(
            src_ref=src, dst_ref=dst, send_sem=send, recv_sem=recv,
            device_id=(group, index), device_id_type=pl.DeviceIdType.MESH,
        )

    def place(j, base, side):
        if col_cuts == 1:
            return pl.ds(pl.multiple_of(base + j * rows, rows), rows), pl.ds(side, cols)
        return (
            pl.ds(pl.multiple_of(base + (j // col_cuts) * rows, rows), rows),
            pl.ds(pl.multiple_of(side + lax.rem(j, col_cuts) * cols, cols), cols),
        )

    def produce(d, scale, store):
        acc[...] = jnp.zeros_like(acc)

        @pl.loop(0, batches)
        def _(k):
            summed = None
            for u in range(batch):
                i = k * batch + u
                value = (dot(env[d], xv[i], NT if d else NN) * scale).astype(bf16)
                if store:
                    keep[i] = value
                term = dot(yv[i], value, NN if d else TN)
                summed = term if summed is None else summed + term
            for h in range(splits):
                acc[h] += summed[:, h * width:(h + 1) * width]

    def part_copy(d, h, j, slot, group):
        at = place(j, 0, 0)
        return remote(stage.at[d, h].at[at[0], at[1]], parts.at[d, h].at[slot], part_send.at[d, h, j],
                      part_recv.at[d, h, slot], group, j * 2 + core)

    def pair_copy(d, h):
        return remote(pair_out.at[d, h], pair_in.at[d, h], pair_send.at[d, h], pair_recv.at[d, h], g, partner)

    def pair_start(d, h):
        other = pl.ds(pl.multiple_of((1 - core) * half, half), half)
        pair_out[d, h] = acc[h, other, :].astype(bf16)
        pair_copy(d, h).start()

    def part_start(d, h, group):
        own = pl.ds(pl.multiple_of(core * half, half), half)
        pair_copy(d, h).wait_recv()
        stage[d, h] = (acc[h, own, :] + pair_in[d, h].astype(f32)).astype(bf16)
        for j in range(chips):
            part_copy(d, h, j, chip, group).start()

    def advance(d, scale, store, group):
        produce(d, scale, store)
        for h in range(splits):
            pair_start(d, h)
        for h in range(splits):
            part_start(d, h, group)

    def finish(d, group):
        for h in range(splits):
            pair_copy(d, h).wait_send()
            for j in range(chips):
                part_copy(d, h, j, chip, group).wait_send()

    def gather_copy(d, h, owner, target):
        at = place(owner, core * half, h * width)
        block = env.at[d].at[at[0], at[1]]
        return remote(block, block, gather_send.at[d, h, target], gather_recv.at[d, h, owner], g, target * 2 + core)

    def relay_copy(d, h, owner, side):
        at = place(owner, side * half, h * width)
        block = env.at[d].at[at[0], at[1]]
        return remote(block, block, relay_send.at[d, h, owner], relay_recv.at[d, h, owner], g, partner)

    def collect(d, group):
        others = [lax.rem(chip + step, chips) for step in range(1, chips)]
        for h in range(splits):
            total = jnp.zeros((rows, cols), f32)
            for j in range(chips):
                part_copy(d, h, 0, j, group).wait_recv()
                total = total + parts[d, h, j].astype(f32)
            at = place(chip, core * half, h * width)
            env[d, at[0], at[1]] = total.astype(bf16)
            for target in others:
                gather_copy(d, h, chip, target).start()
            relay_copy(d, h, chip, core).start()
        for h in range(splits):
            for owner in others:
                gather_copy(d, h, owner, chip).wait_recv()
                relay_copy(d, h, owner, core).start()
        squares = 0.0
        for h in range(splits):
            for j in range(chips):
                relay_copy(d, h, j, 1 - core).wait_recv()
            values = env[d, :, pl.ds(h * width, width)].astype(f32)
            squares = squares + jnp.sum(values * values)
        for h in range(splits):
            for target in others:
                gather_copy(d, h, chip, target).wait_send()
            for j in range(chips):
                relay_copy(d, h, j, core).wait_send()
        return lax.rsqrt(squares / (rank_y * rank_x) + epsilon)

    def out_store(i):
        return pltpu.make_async_copy(outv.at[i], out_hbm.at[i], o_sem.at[i])

    def project(d, scale):
        factor = scale * norm

        @pl.loop(0, batches)
        def _(k):
            group = pl.ds(k * batch, batch)
            if d:
                value = dot(keep[group].reshape(batch * rank_y, rank_x), env[1], NT) * factor
                outv[group] = value.astype(bf16).reshape(batch, rank_y, rank_y)
            else:
                for u in range(batch):
                    outv[k * batch + u] = (dot(env[0], keep[k * batch + u], NT) * factor).astype(bf16)
            for u in range(batch):
                out_store(k * batch + u).start()

        @pl.loop(0, points)
        def _(i):
            out_store(i).wait()

    def run(first, edge, ahead):
        second = 1 - first
        behind = g - (ahead - g)

        @pl.when(g == edge)
        def _():
            bound(first).wait()
            level[0] = 1.0

        @pl.when(g != edge)
        def _():
            level[0] = collect(first, behind)

        advance(first, level[0], True, ahead)
        finish(first, ahead)
        scale = collect(second, ahead)

        @pl.when(g != edge)
        def _():
            advance(second, scale, False, behind)

        project(second, scale)

        @pl.when(g != edge)
        def _():
            finish(second, behind)

    @pl.when(2 * g < groups)
    def _():
        run(0, 0, g + 1)

    @pl.when(2 * g >= groups)
    def _():
        run(1, groups - 1, g - 1)


def body(groups, members, x_cores, y_cores, left_boundary, right_boundary):
    rank_y, rank_x = left_boundary.shape
    points = x_cores.shape[2]
    chips = members // 2
    half, splits, width, rows, cols, col_cuts = cuts(chips, rank_y, rank_x)
    dma = pltpu.SemaphoreType.DMA
    anywhere = pl.BlockSpec(memory_space=pltpu.HBM)
    out = pl.pallas_call(
        functools.partial(kernel, groups, chips),
        out_shape=jax.ShapeDtypeStruct((points, rank_y, rank_y), bf16),
        in_specs=[anywhere] * 4,
        out_specs=anywhere,
        scratch_shapes=[
            pltpu.VMEM((points, rank_y, rank_y), bf16),
            pltpu.VMEM((rank_x, points, rank_x), bf16),
            pltpu.VMEM((rank_y, points, rank_y), bf16),
            pltpu.VMEM((points, rank_x, rank_x), bf16),
            pltpu.VMEM((points, rank_y, rank_y), bf16),
            pltpu.VMEM((points, rank_y, rank_x), bf16),
            pltpu.VMEM((2, rank_y, rank_x), bf16),
            pltpu.VMEM((splits, rank_y, width), f32),
            pltpu.VMEM((2, splits, half, width), bf16),
            pltpu.VMEM((2, splits, half, width), bf16),
            pltpu.VMEM((2, splits, half, width), bf16),
            pltpu.VMEM((2, splits, chips, rows, cols), bf16),
            pltpu.SMEM((1,), f32),
            dma((rank_x // chunk,)), dma((rank_y // chunk,)), dma, dma((points,)), dma((2, splits)), dma((2, splits)),
            dma((2, splits, chips)), dma((2, splits, chips)), dma((2, splits, chips)),
            dma((2, splits, chips)), dma((2, splits, chips)), dma((2, splits, chips)),
        ],
        compiler_params=pltpu.CompilerParams(
            collective_id=0, has_side_effects=True, vmem_limit_bytes=67043328
        ),
    )(x_cores[0], y_cores[0], left_boundary, right_boundary)
    return jnp.transpose(out, (1, 0, 2))[None]


def solution(mesh):
    in_specs = (P("cores", None, "mode", None), P("cores", None, "mode", None), P(), P())
    out_specs = P("cores", None, "mode", None)
    fn = functools.partial(body, mesh.shape["cores"], mesh.shape["mode"])
    return jax.shard_map(fn, mesh=mesh, in_specs=in_specs, out_specs=out_specs, check_vma=False)
```
